512 devices in a mesh: sec: 32 (over z, core), tile: 16 (over x, y).
Axes of the slice: x: 4, y: 4, z: 16, core: 2. Of those that a mesh axis runs over, the one named last changes fastest.
Arguments:
- left_env: bfloat16 [32, 14, 64, 128, 128], P('sec', None, 'tile'), may hold values from -0.5 to 0.5
- right_env: bfloat16 [32, 14, 64, 128, 128], P('sec', None, 'tile'), may hold values from -0.125 to 0.125
- edge_left: bfloat16 [32, 64, 128, 128], P('sec', 'tile'), may hold values from -0.5 to 0.5
- edge_right: bfloat16 [32, 64, 128, 128], P('sec', 'tile'), may hold values from -0.5 to 0.5
- inverse_sv: float32 [32, 64, 128], P('sec', 'tile'), may hold values from 1 to 10
- basis: int32 [32, 64, 128], P('sec', 'tile'), may hold values from 0 to 127, as said below
- lengths: int32 [32, 64], P('sec'), may hold values from 1 to 128, as said below
- partner: int32 [32, 14, 64], P('sec', None, 'tile'), may hold values from 0 to 63, each once within a row
- energy_left: float32 [32, 64, 128], P('sec', 'tile'), may hold values from 0.5 to 2.5
- energy_right: float32 [32, 64, 128], P('sec', 'tile'), may hold values from 0.5 to 2.5
Outputs:
- guess: bfloat16 [32, 64, 128, 128], P('sec', 'tile')
- lanczos_last: bfloat16 [32, 64, 128, 128], P('sec', 'tile')
- tridiag: float32 [32, 8], P('sec')
The draws below stay inside these ranges and needn't reach their ends.
Inputs may be any that keep to these rules, and one draw needn't show every extreme that they name: `lengths`: the 64 sector sizes of each bond sum to 4096; on every bond one sector holds exactly 128 states. `basis`: for a sector of n states, entries 0 to n - 1 are a permutation of 0 to n - 1, and entry a is a for a >= n. `partner`: each channel's row of a bond names every sector once.
All inputs are finite; a program needn't handle non-finite values.
Results may differ from the reference program's by a relative error of at most 0.035.
Values may be sent and summed in bfloat16 or wider, within the bound.
No kernel may reach another device: no remote copies, remote signals or barrier semaphores. Data moves between devices by JAX's collectives and lax.ppermute only.
A program may use at most 64 MiB of HBM per device.

```python
import math
import jax
import jax.numpy as jnp
from jax import lax

S = 64
BMAX = 128
W = 14
ITERS = 4
N_SEC = 32


def size_table(key):
    half_size = BMAX // 2
    first_key, second_key = jax.random.split(key)
    pair_count = (S - 4) // 2
    shifts = jax.random.randint(first_key, (N_SEC, pair_count), -(half_size - 1), half_size, dtype=jnp.int32)
    paired = jnp.stack([half_size + shifts, half_size - shifts], axis=-1).reshape(N_SEC, 2 * pair_count)
    anchors = jnp.broadcast_to(jnp.array([BMAX, 1, half_size - 1, half_size], dtype=jnp.int32), (N_SEC, 4))
    unsorted = jnp.concatenate([anchors, paired], axis=1)
    scores = jax.random.randint(second_key, (N_SEC, S), 0, 1048576, dtype=jnp.int32) * S + jnp.arange(S, dtype=jnp.int32)[None, :]
    positions = jnp.argsort(scores, axis=1)
    return jnp.take_along_axis(unsorted, positions, axis=1).astype(jnp.int32)


def draw_lengths(key, part):
    return size_table(jax.random.fold_in(key, 11))


def draw_basis(key, part):
    sizes_now = size_table(jax.random.fold_in(key, 11))
    slot_index = jnp.arange(BMAX, dtype=jnp.int32)
    alive_slots = slot_index[None, None, :] < sizes_now[:, :, None]
    noise = jax.random.randint(jax.random.fold_in(key, 23), (N_SEC, S, BMAX), 0, 65536, dtype=jnp.int32)
    scores = jnp.where(alive_slots, noise * BMAX + slot_index[None, None, :], 65536 * BMAX + slot_index[None, None, :])
    return jnp.argsort(scores, axis=-1).astype(jnp.int32)


def block_scale(rng, shape, cuts, least, top_value):
    gain = 1.0
    for position, blocks in cuts:
        draws = jax.random.uniform(jax.random.fold_in(jax.random.fold_in(rng, 6), position), (blocks,), jnp.float32, least / len(cuts), top_value / len(cuts))
        gain = gain * jnp.repeat(jnp.exp(draws), shape[position] // blocks).reshape((-1,) + (1,) * (len(shape) - 1 - position))
    return gain


def bell_draw(stream_key, dims, width, reach, cuts=(), held_as=jnp.bfloat16):
    level = block_scale(stream_key, dims, cuts, -0.22, 0.18) if cuts else 1.0
    entries = jax.random.normal(stream_key, dims, jnp.float32) * width * level
    return jnp.minimum(jnp.maximum(entries, -reach), reach).astype(held_as)


def setup_inputs(seed: int = 0) -> dict:
    key_of = jax.random.split(jax.random.key(seed), 11)
    left_env = bell_draw(key_of[0], (N_SEC, W, S, BMAX, BMAX), BMAX ** -0.5, 0.5, ((0, 32), (2, 16)))
    right_env = bell_draw(key_of[1], (N_SEC, W, S, BMAX, BMAX), (W * BMAX) ** -0.5, 0.125, ((0, 32), (2, 16)))
    edge_left = bell_draw(key_of[2], (N_SEC, S, BMAX, BMAX), BMAX ** -0.5, 0.5, ((0, 32), (1, 16)))
    edge_right = bell_draw(key_of[3], (N_SEC, S, BMAX, BMAX), BMAX ** -0.5, 0.5, ((0, 32), (1, 16)))
    inverse_sv = jnp.clip(jnp.exp(math.log(10.0) - 2.3025851 * jax.random.uniform(key_of[4], (N_SEC, S, BMAX), jnp.float32) ** block_scale(key_of[4], (N_SEC, S, BMAX), ((0, 32), (1, 16)), -0.2, 0.2)), 1.0, 10.0)
    basis = draw_basis(jax.random.fold_in(key_of[10], 71), 0)
    lengths = draw_lengths(jax.random.fold_in(key_of[10], 71), 0)
    partner = jax.vmap(lambda own: jax.random.permutation(own, S))(jax.random.split(key_of[7], N_SEC * W)).reshape((N_SEC, W, S)).astype(jnp.int32)
    energy_left = jnp.clip(0.5 + 2.0 * jax.random.uniform(key_of[8], (N_SEC, S, BMAX), jnp.float32) ** block_scale(key_of[8], (N_SEC, S, BMAX), ((0, 32), (1, 16)), -0.2, 0.2), 0.5, 2.5)
    energy_right = jnp.clip(0.5 + 2.0 * jax.random.uniform(key_of[9], (N_SEC, S, BMAX), jnp.float32) ** block_scale(key_of[9], (N_SEC, S, BMAX), ((0, 32), (1, 16)), -0.2, 0.2), 0.5, 2.5)
    return {"left_env": left_env, "right_env": right_env, "edge_left": edge_left, "edge_right": edge_right, "inverse_sv": inverse_sv, "basis": basis, "lengths": lengths, "partner": partner, "energy_left": energy_left, "energy_right": energy_right}


EPSILON = 1e-06

def section_solve(operands):
    left_env, right_env, edge_left, edge_next, inverse_sv, basis, lengths, partner, energy_left, energy_right = operands
    slot_index = jnp.arange(BMAX, dtype=jnp.int32)
    alive_cols = slot_index[None, :] < lengths[:, None]
    live_pair = alive_cols[:, :, None] & alive_cols[:, None, :]
    live_count = jnp.sum(lengths.astype(jnp.float32) ** 2)
    chosen = jnp.take_along_axis(edge_next, basis[:, :, None].astype(jnp.int32), axis=1)
    scaled_left = jnp.where(alive_cols[:, None, :], edge_left.astype(jnp.float32) * inverse_sv[:, None, :], 0.0).astype(jnp.bfloat16)
    merged = jnp.einsum('sab,sbc->sac', scaled_left.astype(jnp.float32), chosen.astype(jnp.float32))
    merged = jnp.where(live_pair, merged, 0.0)
    guess = (merged / jnp.sqrt(jnp.sum(merged * merged) / live_count + EPSILON)).astype(jnp.bfloat16)
    energies = energy_left[:, :, None] + energy_right[:, None, :]
    left_f32 = left_env.astype(jnp.float32)
    right_f32 = right_env.astype(jnp.float32)
    vector = guess
    previous = jnp.zeros_like(guess)
    beta_now = jnp.float32(0.0)
    alphas = []
    betas = []
    for iteration in range(ITERS):
        fetched = vector[partner]
        inner_part = jnp.einsum('wsab,wsbc->wsac', left_f32, fetched.astype(jnp.float32)).astype(jnp.bfloat16)
        coupled = jnp.einsum('wsac,wsdc->sad', inner_part.astype(jnp.float32), right_f32)
        image_all = jnp.where(live_pair, energies * vector.astype(jnp.float32) + coupled, 0.0).astype(jnp.bfloat16)
        present = vector.astype(jnp.float32)
        imaged = image_all.astype(jnp.float32)
        former = previous.astype(jnp.float32)
        alpha_now = jnp.sum(present * imaged) / live_count
        residue = imaged - alpha_now * present - beta_now * former
        beta_next = jnp.sqrt(jnp.sum(residue * residue) / live_count + EPSILON)
        previous = vector
        vector = (residue / beta_next).astype(jnp.bfloat16)
        beta_now = beta_next
        alphas.append(alpha_now)
        betas.append(beta_now)
    return (guess, vector, jnp.stack(alphas + betas))

def reference(left_env, right_env, edge_left, edge_right, inverse_sv, basis, lengths, partner, energy_left, energy_right):
    edge_next = jnp.concatenate([edge_right[1:], edge_right[-1:]], axis=0)
    guess, lanczos_last, tridiag = lax.map(section_solve, (left_env, right_env, edge_left, edge_next, inverse_sv, basis, lengths, partner, energy_left, energy_right))
    return (guess, lanczos_last, tridiag)
```

```python
import functools
import jax
import jax.numpy as jnp
from jax import lax
from jax.experimental import pallas as pl
from jax.experimental.pallas import tpu as pltpu
from jax.sharding import PartitionSpec as P

ITERS = 4
EPSILON = 1e-06
SIDE = 4
TAIL = 16
F32 = jnp.float32
BF16 = jnp.bfloat16
AXES = ("sec", "tile")


def passed_along(value, axis, by):
    peers = lax.axis_size(axis)
    pairs = [(i, i + by) for i in range(peers) if 0 <= i + by < peers]
    return lax.ppermute(value, axis, pairs)


def line_groups(n_sec, stage):
    rows = [[a * SIDE + b for b in range(SIDE)] for a in range(SIDE)]
    cols = [[a * SIDE + b for a in range(SIDE)] for b in range(SIDE)]
    groups = []
    for k in range(n_sec):
        for line in rows if (k % 2 == 0) == (stage == 0) else cols:
            groups.append([k * SIDE * SIDE + i for i in line])
    return groups


def gathered(copies, n_sec):
    rows = copies.shape[1]
    line = lax.all_to_all(copies, AXES, 0, 0, tiled=True, axis_index_groups=line_groups(n_sec, 0))
    line = jnp.broadcast_to(line.reshape(1, SIDE * rows, 128), (SIDE, SIDE * rows, 128))
    whole = lax.all_to_all(line, AXES, 0, 0, tiled=True, axis_index_groups=line_groups(n_sec, 1))
    return whole.reshape(SIDE * SIDE * rows, 128)


def place_of(owner, odd):
    high = owner // SIDE
    low = owner % SIDE
    return jnp.where(odd, low * SIDE + high, owner)


def lane_sums(block):
    return jnp.sum(block, axis=0, keepdims=True)


def in_pieces(sums):
    row = lax.broadcasted_iota(jnp.int32, (TAIL, 128), 0)
    out = jnp.zeros((TAIL, 128), F32)
    for q, value in enumerate(sums):
        for k in range(3):
            piece = value.astype(BF16).astype(F32)
            out = jnp.where(row == 3 * q + k, piece, out)
            value = value - piece
    return out.astype(BF16)


def totals(whole_ref, n_dev, rows, n_sums):
    acc = jnp.zeros((TAIL, 128), F32)
    for i in range(n_dev):
        acc = acc + whole_ref[i * rows + rows - TAIL : (i + 1) * rows, :].astype(F32)
    out = []
    for q in range(n_sums):
        lanes = jnp.sum(acc[3 * q : 3 * q + 3, :], axis=0, keepdims=True)
        out.append(jnp.sum(lanes, axis=1, keepdims=True))
    return out


def merge_body(per, lengths_s, lengths_v, own_edge, sent_edge, left, inv, basis, e_left, e_right,
               out_ref, energy_ref, merged_ref, state_ref):
    at_end = lax.axis_index("sec") == lax.axis_size("sec") - 1
    first = lax.axis_index("tile") * per
    row = lax.broadcasted_iota(jnp.int32, (128, 128), 0)
    col = lax.broadcasted_iota(jnp.int32, (128, 128), 1)
    squares = jnp.zeros((1, 128), F32)
    weighted = jnp.zeros((1, 128), F32)
    for s in range(per):
        n = lengths_s[0, first + s]
        live = (row < n) & (col < n)
        scaled = jnp.where(col < n, left[0, s].astype(F32) * inv[0, s : s + 1, :], 0.0).astype(BF16)
        pick = jnp.where(row == basis[0, s : s + 1, :], 1.0, 0.0).astype(BF16)
        moved = lax.dot_general(scaled, pick, (((1,), (1,)), ((), ())), preferred_element_type=F32)
        following = jnp.where(at_end, own_edge[0, s].astype(F32), sent_edge[0, s].astype(F32)).astype(BF16)
        merged = jnp.dot(moved.astype(BF16), following, preferred_element_type=F32)
        merged = jnp.where(live, merged, 0.0)
        e_rows = jnp.broadcast_to(e_left[0, s : s + 1, :], (128, 128)).T
        energy = jnp.where(live, e_rows + e_right[0, s : s + 1, :], 0.0)
        energy_ref[s] = energy
        merged_ref[s] = merged
        blocks = merged.astype(BF16)
        for k in range(SIDE):
            out_ref[k, s * 128 : (s + 1) * 128, :] = blocks
        square = merged * merged
        squares = squares + lane_sums(square)
        weighted = weighted + lane_sums(square * energy)
    tail = in_pieces([squares, weighted])
    for k in range(SIDE):
        out_ref[k, per * 128 : per * 128 + TAIL, :] = tail
    sizes = lengths_v[...].astype(F32)
    count = jnp.sum(sizes * sizes, axis=1, keepdims=True)
    state_ref[...] = jnp.zeros((16, 128), F32)
    state_ref[0:1, :] = jnp.broadcast_to(1.0 / count, (1, 128))


def coupled(per, n_w, s, whole, left, right, partner, odd, rows):
    def fetched(w):
        sector = partner[s, w]
        at = place_of(sector // per, odd) * rows + (sector % per) * 128
        return whole[pl.ds(pl.multiple_of(at, 16), 128), :]

    acc = jnp.zeros((128, 128), F32)
    for w in range(0, n_w, 2):
        inner = [
            jnp.dot(left[0, w + i, s], fetched(w + i), preferred_element_type=F32).astype(BF16)
            for i in range(2)
        ]
        acc = acc + lax.dot_general(
            jnp.concatenate(inner, axis=1),
            jnp.concatenate([right[0, w, s], right[0, w + 1, s]], axis=1),
            (((1,), (1,)), ((), ())),
            preferred_element_type=F32,
        )
    return acc


def step_body(step, per, n_w, n_dev, partner, whole, left, right, energy_ref, state_in, *refs):
    if step == 0:
        merged_ref, guess_ref, out_ref, vector_ref, image_ref, state_ref = refs
    elif step < ITERS - 1:
        v_prev, image_prev, out_ref, vector_ref, image_ref, state_ref = refs
    else:
        v_prev, image_prev, sums_ref, ahead_ref, vector_ref, state_ref = refs
    rows = per * 128 + TAIL
    odd = lax.axis_index("sec") % 2 == 1
    own = place_of(lax.axis_index("tile"), odd) * rows
    inv_count = state_in[0:1, 0:1]
    state = [state_in[k : k + 1, :] for k in range(16)]
    if step == 0:
        square, weighted = totals(whole, n_dev, rows, 2)
        over = 1.0 / jnp.sqrt(square * inv_count + EPSILON)
        shift = weighted * over * over * inv_count
    else:
        a, b, c, d = totals(whole, n_dev, rows, 4)
        alpha = a * inv_count
        late = alpha - state_in[1:2, 0:1]
        norm = jnp.maximum(b - 2.0 * late * c + late * late * d, 0.0)
        beta = jnp.sqrt(norm * inv_count + EPSILON)
        over = 1.0 / beta
        shift = alpha
        state[1 + step] = jnp.broadcast_to(alpha, (1, 128))
        state[5 + step] = jnp.broadcast_to(beta, (1, 128))
    state[1] = jnp.broadcast_to(shift, (1, 128))
    for k in range(16):
        state_ref[k : k + 1, :] = state[k]
    sums = [jnp.zeros((1, 128), F32) for _ in range(4)]
    for s in range(per):
        present = whole[pl.ds(pl.multiple_of(own + s * 128, 16), 128), :].astype(F32)
        energy = energy_ref[s]
        acc = coupled(per, n_w, s, whole, left, right, partner, odd, rows)
        image = jnp.where(energy > 0.0, energy * present + acc, 0.0)
        if step == 0:
            guess_ref[0, s] = (merged_ref[s] * over).astype(BF16)
            image = image * over
            vector = present * over
            ahead = image - shift * vector
        else:
            image = (image - late * image_prev[s]) * over
            vector = (present - late * v_prev[s]) * over
            ahead = image - shift * vector - beta * v_prev[s]
        sums[0] = sums[0] + lane_sums(vector * image)
        sums[1] = sums[1] + lane_sums(ahead * ahead)
        sums[2] = sums[2] + lane_sums(ahead * vector)
        sums[3] = sums[3] + lane_sums(vector * vector)
        vector_ref[s] = vector
        if step < ITERS - 1:
            image_ref[s] = image
            blocks = ahead.astype(BF16)
            for k in range(SIDE):
                out_ref[k, s * 128 : (s + 1) * 128, :] = blocks
        else:
            ahead_ref[s] = ahead
    if step < ITERS - 1:
        tail = in_pieces(sums)
        for k in range(SIDE):
            out_ref[k, per * 128 : per * 128 + TAIL, :] = tail
    else:
        for k in range(n_dev):
            for q in range(4):
                sums_ref[k, q : q + 1, :] = sums[q]
            sums_ref[k, 4:8, :] = jnp.zeros((4, 128), F32)


def last_body(per, n_dev, sums_ref, ahead_ref, v_prev, state_in, out_ref, tridiag_ref):
    acc = sums_ref[0]
    for k in range(1, n_dev):
        acc = acc + sums_ref[k]
    a, b, c, d = (jnp.sum(acc[q : q + 1, :], axis=1, keepdims=True) for q in range(4))
    inv_count = state_in[0:1, 0:1]
    alpha = a * inv_count
    late = alpha - state_in[1:2, 0:1]
    norm = jnp.maximum(b - 2.0 * late * c + late * late * d, 0.0)
    beta = jnp.sqrt(norm * inv_count + EPSILON)
    over = 1.0 / beta
    for s in range(per):
        out_ref[0, s] = ((ahead_ref[s] - late * v_prev[s]) * over).astype(BF16)
    lane = lax.broadcasted_iota(jnp.int32, (1, 128), 1)
    values = [state_in[2 + k : 3 + k, :] for k in range(3)] + [alpha]
    values += [state_in[6 + k : 7 + k, :] for k in range(3)] + [beta]
    line = jnp.zeros((1, 128), F32)
    for k, value in enumerate(values):
        line = jnp.where(lane == k, value, line)
    tridiag_ref[...] = line[:, :8]


def call(body, outs, n_smem, operands, name):
    vmem = pl.BlockSpec(memory_space=pltpu.VMEM)
    smem = pl.BlockSpec(memory_space=pltpu.SMEM)
    return pl.pallas_call(
        body,
        out_shape=[jax.ShapeDtypeStruct(shape, dtype) for shape, dtype in outs],
        in_specs=[smem] * n_smem + [vmem] * (len(operands) - n_smem),
        out_specs=[vmem] * len(outs),
        compiler_params=pltpu.CompilerParams(vmem_limit_bytes=24 << 20),
        name=name,
    )(*operands)


def on_device(
    n_sec,
    n_dev,
    left_env,
    right_env,
    edge_left,
    edge_right,
    inverse_sv,
    basis,
    lengths,
    partner,
    energy_left,
    energy_right,
):
    per = edge_left.shape[1]
    n_w = left_env.shape[1]
    rows = per * 128 + TAIL
    sent_edge = passed_along(edge_right, "sec", -1)
    routes = jnp.swapaxes(partner, 1, 2)[0]
    cube = ((per, 128, 128), F32)
    small = ((16, 128), F32)
    copies = ((SIDE, rows, 128), BF16)
    send, energy, merged, state = call(
        functools.partial(merge_body, per),
        [copies, cube, cube, small],
        1,
        (lengths, lengths, edge_right, sent_edge, edge_left, inverse_sv, basis, energy_left, energy_right),
        "merge",
    )
    for step in range(ITERS):
        whole = gathered(send, n_sec)
        body = functools.partial(step_body, step, per, n_w, n_dev)
        common = (routes, whole, left_env, right_env, energy, state)
        if step == 0:
            guess, send, vector, image, state = call(
                body,
                [((1, per, 128, 128), BF16), copies, cube, cube, small],
                1,
                common + (merged,),
                "step_first",
            )
        elif step < ITERS - 1:
            send, vector, image, state = call(
                body, [copies, cube, cube, small], 1, common + (vector, image), "step_next"
            )
        else:
            sums, ahead, vector, state = call(
                body,
                [((n_dev, 8, 128), F32), cube, cube, small],
                1,
                common + (vector, image),
                "step_last",
            )
    sums = lax.all_to_all(sums, "tile", 0, 0, tiled=True)
    last, tridiag = call(
        functools.partial(last_body, per, n_dev),
        [((1, per, 128, 128), BF16), ((1, 8), F32)],
        0,
        (sums, ahead, vector, state),
        "finish",
    )
    return guess, last, tridiag


def solution(mesh):
    placed = (
        P("sec", None, "tile", None, None),
        P("sec", None, "tile", None, None),
        P("sec", "tile", None, None),
        P("sec", "tile", None, None),
        P("sec", "tile", None),
        P("sec", "tile", None),
        P("sec", None),
        P("sec", None, "tile"),
        P("sec", "tile", None),
        P("sec", "tile", None),
    )
    return jax.shard_map(
        functools.partial(on_device, mesh.shape["sec"], mesh.shape["tile"]),
        mesh=mesh,
        in_specs=placed,
        out_specs=(P("sec", "tile", None, None), P("sec", "tile", None, None), P("sec", None)),
        check_vma=False,
    )
```

```python
import functools
import jax
import jax.numpy as jnp
from jax import lax
from jax.experimental import pallas as pl
from jax.experimental.pallas import tpu as pltpu
from jax.sharding import PartitionSpec as P

ITERS = 4
EPSILON = 1e-06
SIDE = 4
TAIL = 16
F32 = jnp.float32
BF16 = jnp.bfloat16
AXES = ("sec", "tile")


def passed_along(value, axis, by):
    peers = lax.axis_size(axis)
    pairs = [(i, i + by) for i in range(peers) if 0 <= i + by < peers]
    return lax.ppermute(value, axis, pairs)


def line_groups(n_sec, stage):
    rows = [[a * SIDE + b for b in range(SIDE)] for a in range(SIDE)]
    cols = [[a * SIDE + b for a in range(SIDE)] for b in range(SIDE)]
    groups = []
    for k in range(n_sec):
        for line in rows if (k % 2 == 0) == (stage == 0) else cols:
            groups.append([k * SIDE * SIDE + i for i in line])
    return groups


def gathered(copies, n_sec):
    rows = copies.shape[1]
    line = lax.all_to_all(copies, AXES, 0, 0, tiled=True, axis_index_groups=line_groups(n_sec, 0))
    line = jnp.broadcast_to(line.reshape(1, SIDE * rows, 128), (SIDE, SIDE * rows, 128))
    whole = lax.all_to_all(line, AXES, 0, 0, tiled=True, axis_index_groups=line_groups(n_sec, 1))
    return whole.reshape(SIDE * SIDE * rows, 128)


def place_of(owner, odd):
    high = owner // SIDE
    low = owner % SIDE
    return jnp.where(odd, low * SIDE + high, owner)


def lane_sums(block):
    return jnp.sum(block, axis=0, keepdims=True)


def in_pieces(sums):
    row = lax.broadcasted_iota(jnp.int32, (TAIL, 128), 0)
    out = jnp.zeros((TAIL, 128), F32)
    for q, value in enumerate(sums):
        for k in range(3):
            piece = value.astype(BF16).astype(F32)
            out = jnp.where(row == 3 * q + k, piece, out)
            value = value - piece
    return out.astype(BF16)


def totals(whole_ref, n_dev, rows, n_sums):
    acc = jnp.zeros((TAIL, 128), F32)
    for i in range(n_dev):
        acc = acc + whole_ref[i * rows + rows - TAIL : (i + 1) * rows, :].astype(F32)
    out = []
    for q in range(n_sums):
        lanes = jnp.sum(acc[3 * q : 3 * q + 3, :], axis=0, keepdims=True)
        out.append(jnp.sum(lanes, axis=1, keepdims=True))
    return out


def prepare_body(per, n_w, lengths, partner, own_edge, left, inv, basis, e_left, e_right,
                 moved_ref, own_ref, energy_ref, state_ref, places_ref,
                 lengths_s, partner_s, lengths_v, left_v, inv_v, basis_v, e_left_v, e_right_v, sems):
    pairs = [
        (lengths, lengths_s),
        (partner, partner_s),
        (lengths, lengths_v),
        (basis, basis_v),
        (inv, inv_v),
        (e_left, e_left_v),
        (e_right, e_right_v),
        (left, left_v),
        (own_edge, own_ref),
    ]
    copies = [pltpu.make_async_copy(src, dst, sems.at[k]) for k, (src, dst) in enumerate(pairs)]
    for copy in copies:
        copy.start()
    for copy in copies:
        copy.wait()
    rows = per * 128 + TAIL
    odd = lax.axis_index("sec") % 2 == 1
    for s in range(per):
        for w in range(n_w):
            sector = partner_s[s, w]
            places_ref[s, w] = place_of(sector // per, odd) * rows + (sector % per) * 128
    first = lax.axis_index("tile") * per
    row = lax.broadcasted_iota(jnp.int32, (128, 128), 0)
    col = lax.broadcasted_iota(jnp.int32, (128, 128), 1)
    for s in range(per):
        n = lengths_s[0, first + s]
        scaled = jnp.where(col < n, left_v[0, s].astype(F32) * inv_v[0, s : s + 1, :], 0.0).astype(BF16)
        pick = jnp.where(row == basis_v[0, s : s + 1, :], 1.0, 0.0).astype(BF16)
        moved = lax.dot_general(scaled, pick, (((1,), (1,)), ((), ())), preferred_element_type=F32)
        moved_ref[s] = moved.astype(BF16)
        e_rows = jnp.broadcast_to(e_left_v[0, s : s + 1, :], (128, 128)).T
        energy_ref[s] = jnp.where((row < n) & (col < n), e_rows + e_right_v[0, s : s + 1, :], 0.0)
    sizes = lengths_v[...].astype(F32)
    count = jnp.sum(sizes * sizes, axis=1, keepdims=True)
    state_ref[...] = jnp.broadcast_to(1.0 / count, (16, 128))


def merge_body(per, sent_edge, own_edge, moved_ref, energy_ref, out_ref, merged_ref):
    at_end = lax.axis_index("sec") == lax.axis_size("sec") - 1
    squares = jnp.zeros((1, 128), F32)
    weighted = jnp.zeros((1, 128), F32)
    for s in range(per):
        following = jnp.where(at_end, own_edge[0, s].astype(F32), sent_edge[0, s].astype(F32)).astype(BF16)
        energy = energy_ref[s]
        merged = jnp.dot(moved_ref[s], following, preferred_element_type=F32)
        merged = jnp.where(energy > 0.0, merged, 0.0)
        merged_ref[s] = merged
        blocks = merged.astype(BF16)
        for k in range(SIDE):
            out_ref[k, s * 128 : (s + 1) * 128, :] = blocks
        square = merged * merged
        squares = squares + lane_sums(square)
        weighted = weighted + lane_sums(square * energy)
    tail = in_pieces([squares, weighted])
    for k in range(SIDE):
        out_ref[k, per * 128 : per * 128 + TAIL, :] = tail


def coupled(n_w, s, whole, left, right, places):
    def fetched(w):
        return whole[pl.ds(pl.multiple_of(places[s, w], 16), 128), :]

    acc = jnp.zeros((128, 128), F32)
    for w in range(0, n_w, 2):
        inner = [
            jnp.dot(left[0, w + i, s], fetched(w + i), preferred_element_type=F32).astype(BF16)
            for i in range(2)
        ]
        acc = acc + lax.dot_general(
            jnp.concatenate(inner, axis=1),
            jnp.concatenate([right[0, w, s], right[0, w + 1, s]], axis=1),
            (((1,), (1,)), ((), ())),
            preferred_element_type=F32,
        )
    return acc


def step_body(step, per, n_w, n_dev, places, whole, left, right, energy_ref, state_in, *refs):
    if step == 0:
        merged_ref, guess_ref, out_ref, vector_ref, image_ref, state_ref, guess_v, guess_sem = refs
    elif step < ITERS - 1:
        v_prev, image_prev, out_ref, vector_ref, image_ref, state_ref = refs
    else:
        v_prev, image_prev, sums_ref, ahead_ref, vector_ref, state_ref = refs
    rows = per * 128 + TAIL
    odd = lax.axis_index("sec") % 2 == 1
    own = place_of(lax.axis_index("tile"), odd) * rows
    inv_count = state_in[0:1, 0:1]
    state = [state_in[k : k + 1, :] for k in range(16)]
    if step == 0:
        square, weighted = totals(whole, n_dev, rows, 2)
        over = 1.0 / jnp.sqrt(square * inv_count + EPSILON)
        shift = weighted * over * over * inv_count
        for s in range(per):
            guess_v[0, s] = (merged_ref[s] * over).astype(BF16)
        guess_copy = pltpu.make_async_copy(guess_v, guess_ref, guess_sem)
        guess_copy.start()
    else:
        a, b, c, d = totals(whole, n_dev, rows, 4)
        alpha = a * inv_count
        late = alpha - state_in[1:2, 0:1]
        norm = jnp.maximum(b - 2.0 * late * c + late * late * d, 0.0)
        beta = jnp.sqrt(norm * inv_count + EPSILON)
        over = 1.0 / beta
        shift = alpha
        state[1 + step] = jnp.broadcast_to(alpha, (1, 128))
        state[5 + step] = jnp.broadcast_to(beta, (1, 128))
    state[1] = jnp.broadcast_to(shift, (1, 128))
    for k in range(16):
        state_ref[k : k + 1, :] = state[k]
    sums = [jnp.zeros((1, 128), F32) for _ in range(4)]
    for s in range(per):
        present = whole[pl.ds(pl.multiple_of(own + s * 128, 16), 128), :].astype(F32)
        energy = energy_ref[s]
        acc = coupled(n_w, s, whole, left, right, places)
        image = jnp.where(energy > 0.0, energy * present + acc, 0.0)
        if step == 0:
            image = image * over
            vector = present * over
            ahead = image - shift * vector
        else:
            image = (image - late * image_prev[s]) * over
            vector = (present - late * v_prev[s]) * over
            ahead = image - shift * vector - beta * v_prev[s]
        sums[0] = sums[0] + lane_sums(vector * image)
        sums[1] = sums[1] + lane_sums(ahead * ahead)
        sums[2] = sums[2] + lane_sums(ahead * vector)
        sums[3] = sums[3] + lane_sums(vector * vector)
        vector_ref[s] = vector
        if step < ITERS - 1:
            image_ref[s] = image
            blocks = ahead.astype(BF16)
            for k in range(SIDE):
                out_ref[k, s * 128 : (s + 1) * 128, :] = blocks
        else:
            ahead_ref[s] = ahead
    if step < ITERS - 1:
        tail = in_pieces(sums)
        for k in range(SIDE):
            out_ref[k, per * 128 : per * 128 + TAIL, :] = tail
    else:
        for k in range(n_dev):
            for q in range(4):
                sums_ref[k, q : q + 1, :] = sums[q]
            sums_ref[k, 4:8, :] = jnp.zeros((4, 128), F32)
    if step == 0:
        guess_copy.wait()


def last_body(per, n_dev, sums_ref, ahead_ref, v_prev, state_in, out_ref, tridiag_ref):
    acc = sums_ref[0]
    for k in range(1, n_dev):
        acc = acc + sums_ref[k]
    a, b, c, d = (jnp.sum(acc[q : q + 1, :], axis=1, keepdims=True) for q in range(4))
    inv_count = state_in[0:1, 0:1]
    alpha = a * inv_count
    late = alpha - state_in[1:2, 0:1]
    norm = jnp.maximum(b - 2.0 * late * c + late * late * d, 0.0)
    beta = jnp.sqrt(norm * inv_count + EPSILON)
    over = 1.0 / beta
    for s in range(per):
        out_ref[0, s] = ((ahead_ref[s] - late * v_prev[s]) * over).astype(BF16)
    lane = lax.broadcasted_iota(jnp.int32, (1, 128), 1)
    values = [state_in[2 + k : 3 + k, :] for k in range(3)] + [alpha]
    values += [state_in[6 + k : 7 + k, :] for k in range(3)] + [beta]
    line = jnp.zeros((1, 128), F32)
    for k, value in enumerate(values):
        line = jnp.where(lane == k, value, line)
    tridiag_ref[...] = line[:, :8]


VMEM = pl.BlockSpec(memory_space=pltpu.VMEM)
SMEM = pl.BlockSpec(memory_space=pltpu.SMEM)
HBM = pl.BlockSpec(memory_space=pltpu.HBM)


def call(body, outs, operands, name, scratch=()):
    return pl.pallas_call(
        body,
        out_shape=[jax.ShapeDtypeStruct(shape, dtype) for _, shape, dtype in outs],
        in_specs=[spec for spec, _ in operands],
        out_specs=[spec for spec, _, _ in outs],
        scratch_shapes=list(scratch),
        compiler_params=pltpu.CompilerParams(vmem_limit_bytes=24 << 20),
        name=name,
    )(*[array for _, array in operands])


def on_device(
    n_sec,
    n_dev,
    left_env,
    right_env,
    edge_left,
    edge_right,
    inverse_sv,
    basis,
    lengths,
    partner,
    energy_left,
    energy_right,
):
    per = edge_left.shape[1]
    n_w = left_env.shape[1]
    rows = per * 128 + TAIL
    cube = (VMEM, (per, 128, 128), F32)
    small = (VMEM, (16, 128), F32)
    copies = (VMEM, (SIDE, rows, 128), BF16)
    edge = (1, per, 128, 128)
    sent_edge = passed_along(edge_right, "sec", -1)
    routes = jnp.swapaxes(partner, 1, 2)[0]
    given = (lengths, routes, edge_right, edge_left, inverse_sv, basis, energy_left, energy_right)
    line = (1, per, 128)
    moved, own_edge, energy, state, places = call(
        functools.partial(prepare_body, per, n_w),
        [(VMEM, (per, 128, 128), BF16), (VMEM, edge, BF16), cube, small, (SMEM, (per, n_w), jnp.int32)],
        [(HBM, pltpu.with_memory_space_constraint(array, pltpu.HBM)) for array in given],
        "prepare",
        [
            pltpu.SMEM(lengths.shape, jnp.int32),
            pltpu.SMEM((per, n_w), jnp.int32),
            pltpu.VMEM(lengths.shape, jnp.int32),
            pltpu.VMEM(edge, BF16),
            pltpu.VMEM(line, F32),
            pltpu.VMEM(line, jnp.int32),
            pltpu.VMEM(line, F32),
            pltpu.VMEM(line, F32),
            pltpu.SemaphoreType.DMA((9,)),
        ],
    )
    send, merged = call(
        functools.partial(merge_body, per),
        [copies, cube],
        [(VMEM, sent_edge), (VMEM, own_edge), (VMEM, moved), (VMEM, energy)],
        "merge",
    )
    for step in range(ITERS):
        whole = gathered(send, n_sec)
        body = functools.partial(step_body, step, per, n_w, n_dev)
        common = [(SMEM, places)]
        common += [(VMEM, array) for array in (whole, left_env, right_env, energy, state)]
        if step == 0:
            guess, send, vector, image, state = call(
                body,
                [(HBM, edge, BF16), copies, cube, cube, small],
                common + [(VMEM, merged)],
                "step_first",
                [pltpu.VMEM(edge, BF16), pltpu.SemaphoreType.DMA],
            )
        elif step < ITERS - 1:
            send, vector, image, state = call(
                body,
                [copies, cube, cube, small],
                common + [(VMEM, vector), (VMEM, image)],
                "step_next",
            )
        else:
            sums, ahead, vector, state = call(
                body,
                [(VMEM, (n_dev, 8, 128), F32), cube, cube, small],
                common + [(VMEM, vector), (VMEM, image)],
                "step_last",
            )
    sums = lax.all_to_all(sums, "tile", 0, 0, tiled=True)
    last, tridiag = call(
        functools.partial(last_body, per, n_dev),
        [(VMEM, edge, BF16), (VMEM, (1, 8), F32)],
        [(VMEM, array) for array in (sums, ahead, vector, state)],
        "finish",
    )
    return guess, last, tridiag


def solution(mesh):
    placed = (
        P("sec", None, "tile", None, None),
        P("sec", None, "tile", None, None),
        P("sec", "tile", None, None),
        P("sec", "tile", None, None),
        P("sec", "tile", None),
        P("sec", "tile", None),
        P("sec", None),
        P("sec", None, "tile"),
        P("sec", "tile", None),
        P("sec", "tile", None),
    )
    return jax.shard_map(
        functools.partial(on_device, mesh.shape["sec"], mesh.shape["tile"]),
        mesh=mesh,
        in_specs=placed,
        out_specs=(P("sec", "tile", None, None), P("sec", "tile", None, None), P("sec", None)),
        check_vma=False,
    )
```

```python
import functools
import jax
import jax.numpy as jnp
from jax import lax
from jax.experimental import pallas as pl
from jax.experimental.pallas import tpu as pltpu
from jax.sharding import PartitionSpec as P

ITERS = 4
EPSILON = 1e-06
SIDE = 4
TAIL = 16
F32 = jnp.float32
BF16 = jnp.bfloat16
AXES = ("sec", "tile")


def passed_along(value, axis, by):
    peers = lax.axis_size(axis)
    pairs = [(i, i + by) for i in range(peers) if 0 <= i + by < peers]
    return lax.ppermute(value, axis, pairs)


def line_groups(n_sec, stage):
    rows = [[a * SIDE + b for b in range(SIDE)] for a in range(SIDE)]
    cols = [[a * SIDE + b for a in range(SIDE)] for b in range(SIDE)]
    groups = []
    for k in range(n_sec):
        for line in rows if (k % 2 == 0) == (stage == 0) else cols:
            groups.append([k * SIDE * SIDE + i for i in line])
    return groups


def gathered(copies, n_sec):
    rows = copies.shape[1]
    line = lax.all_to_all(copies, AXES, 0, 0, tiled=True, axis_index_groups=line_groups(n_sec, 0))
    line = jnp.broadcast_to(line.reshape(1, SIDE * rows, 128), (SIDE, SIDE * rows, 128))
    whole = lax.all_to_all(line, AXES, 0, 0, tiled=True, axis_index_groups=line_groups(n_sec, 1))
    return whole.reshape(SIDE * SIDE * rows, 128)


def place_of(owner, odd):
    high = owner // SIDE
    low = owner % SIDE
    return jnp.where(odd, low * SIDE + high, owner)


def lane_sums(block):
    return jnp.sum(block, axis=0, keepdims=True)


def in_pieces(sums):
    row = lax.broadcasted_iota(jnp.int32, (TAIL, 128), 0)
    out = jnp.zeros((TAIL, 128), F32)
    for q, value in enumerate(sums):
        for k in range(3):
            piece = value.astype(BF16).astype(F32)
            out = jnp.where(row == 3 * q + k, piece, out)
            value = value - piece
    return out.astype(BF16)


def totals(whole_ref, n_dev, rows, n_sums):
    acc = jnp.zeros((TAIL, 128), F32)
    for i in range(n_dev):
        acc = acc + whole_ref[i * rows + rows - TAIL : (i + 1) * rows, :].astype(F32)
    out = []
    for q in range(n_sums):
        lanes = jnp.sum(acc[3 * q : 3 * q + 3, :], axis=0, keepdims=True)
        out.append(jnp.sum(lanes, axis=1, keepdims=True))
    return out


def prepare_body(per, n_w, lengths, partner, own_edge, left, inv, basis, e_left, e_right,
                 moved_ref, own_ref, energy_ref, state_ref, places_ref,
                 lengths_s, partner_s, lengths_v, left_v, inv_v, basis_v, e_left_v, e_right_v, sems):
    pairs = [
        (lengths, lengths_s),
        (partner, partner_s),
        (lengths, lengths_v),
        (basis, basis_v),
        (inv, inv_v),
        (e_left, e_left_v),
        (e_right, e_right_v),
        (left, left_v),
        (own_edge, own_ref),
    ]
    copies = [pltpu.make_async_copy(src, dst, sems.at[k]) for k, (src, dst) in enumerate(pairs)]
    for copy in copies:
        copy.start()
    for copy in copies:
        copy.wait()
    rows = per * 128 + TAIL
    odd = lax.axis_index("sec") % 2 == 1
    for s in range(per):
        for w in range(n_w):
            sector = partner_s[s, w]
            places_ref[s, w] = place_of(sector // per, odd) * rows + (sector % per) * 128
    first = lax.axis_index("tile") * per
    row = lax.broadcasted_iota(jnp.int32, (128, 128), 0)
    col = lax.broadcasted_iota(jnp.int32, (128, 128), 1)
    for s in range(per):
        n = lengths_s[0, first + s]
        scaled = jnp.where(col < n, left_v[0, s].astype(F32) * inv_v[0, s : s + 1, :], 0.0).astype(BF16)
        pick = jnp.where(row == basis_v[0, s : s + 1, :], 1.0, 0.0).astype(BF16)
        moved = lax.dot_general(scaled, pick, (((1,), (1,)), ((), ())), preferred_element_type=F32)
        moved_ref[s] = moved.astype(BF16)
        e_rows = jnp.broadcast_to(e_left_v[0, s : s + 1, :], (128, 128)).T
        energy_ref[s] = jnp.where((row < n) & (col < n), e_rows + e_right_v[0, s : s + 1, :], 0.0)
    sizes = lengths_v[...].astype(F32)
    count = jnp.sum(sizes * sizes, axis=1, keepdims=True)
    state_ref[...] = jnp.broadcast_to(1.0 / count, (16, 128))


def merge_body(per, sent_edge, own_edge, moved_ref, energy_ref, out_ref, merged_ref):
    at_end = lax.axis_index("sec") == lax.axis_size("sec") - 1
    squares = jnp.zeros((1, 128), F32)
    weighted = jnp.zeros((1, 128), F32)
    for s in range(per):
        following = jnp.where(at_end, own_edge[0, s].astype(F32), sent_edge[0, s].astype(F32)).astype(BF16)
        energy = energy_ref[s]
        merged = jnp.dot(moved_ref[s], following, preferred_element_type=F32)
        merged = jnp.where(energy > 0.0, merged, 0.0)
        merged_ref[s] = merged
        blocks = merged.astype(BF16)
        for k in range(SIDE):
            out_ref[k, s * 128 : (s + 1) * 128, :] = blocks
        square = merged * merged
        squares = squares + lane_sums(square)
        weighted = weighted + lane_sums(square * energy)
    tail = in_pieces([squares, weighted])
    for k in range(SIDE):
        out_ref[k, per * 128 : per * 128 + TAIL, :] = tail


def coupled(n_w, s, whole, left, right, places):
    def fetched(w):
        return whole[pl.ds(pl.multiple_of(places[s, w], 16), 128), :]

    inner = [
        jnp.dot(left[0, w, s], fetched(w), preferred_element_type=F32).astype(BF16) for w in range(n_w)
    ]
    return lax.dot_general(
        jnp.concatenate(inner, axis=1),
        jnp.concatenate([right[0, w, s] for w in range(n_w)], axis=1),
        (((1,), (1,)), ((), ())),
        preferred_element_type=F32,
    )


def step_body(step, per, n_w, n_dev, places, whole, left, right, energy_ref, state_in, *refs):
    if step == 0:
        merged_ref, guess_ref, out_ref, vector_ref, image_ref, state_ref = refs
    elif step < ITERS - 1:
        v_prev, image_prev, out_ref, vector_ref, image_ref, state_ref = refs
    else:
        v_prev, image_prev, sums_ref, ahead_ref, vector_ref, state_ref = refs
    rows = per * 128 + TAIL
    odd = lax.axis_index("sec") % 2 == 1
    own = place_of(lax.axis_index("tile"), odd) * rows
    inv_count = state_in[0:1, 0:1]
    state = [state_in[k : k + 1, :] for k in range(16)]
    if step == 0:
        square, weighted = totals(whole, n_dev, rows, 2)
        over = 1.0 / jnp.sqrt(square * inv_count + EPSILON)
        shift = weighted * over * over * inv_count
        for s in range(per):
            guess_ref[0, s] = (merged_ref[s] * over).astype(BF16)
    else:
        a, b, c, d = totals(whole, n_dev, rows, 4)
        alpha = a * inv_count
        late = alpha - state_in[1:2, 0:1]
        norm = jnp.maximum(b - 2.0 * late * c + late * late * d, 0.0)
        beta = jnp.sqrt(norm * inv_count + EPSILON)
        over = 1.0 / beta
        shift = alpha
        state[1 + step] = jnp.broadcast_to(alpha, (1, 128))
        state[5 + step] = jnp.broadcast_to(beta, (1, 128))
    state[1] = jnp.broadcast_to(shift, (1, 128))
    for k in range(16):
        state_ref[k : k + 1, :] = state[k]
    sums = [jnp.zeros((1, 128), F32) for _ in range(4)]
    for s in range(per):
        present = whole[pl.ds(pl.multiple_of(own + s * 128, 16), 128), :].astype(F32)
        energy = energy_ref[s]
        acc = coupled(n_w, s, whole, left, right, places)
        image = jnp.where(energy > 0.0, energy * present + acc, 0.0)
        if step == 0:
            image = image * over
            vector = present * over
            ahead = image - shift * vector
        else:
            image = (image - late * image_prev[s]) * over
            vector = (present - late * v_prev[s]) * over
            ahead = image - shift * vector - beta * v_prev[s]
        sums[0] = sums[0] + lane_sums(vector * image)
        sums[1] = sums[1] + lane_sums(ahead * ahead)
        sums[2] = sums[2] + lane_sums(ahead * vector)
        sums[3] = sums[3] + lane_sums(vector * vector)
        vector_ref[s] = vector
        if step < ITERS - 1:
            image_ref[s] = image
            blocks = ahead.astype(BF16)
            for k in range(SIDE):
                out_ref[k, s * 128 : (s + 1) * 128, :] = blocks
        else:
            ahead_ref[s] = ahead
    if step < ITERS - 1:
        tail = in_pieces(sums)
        for k in range(SIDE):
            out_ref[k, per * 128 : per * 128 + TAIL, :] = tail
    else:
        for k in range(n_dev):
            for q in range(4):
                sums_ref[k, q : q + 1, :] = sums[q]
            sums_ref[k, 4:8, :] = jnp.zeros((4, 128), F32)


def last_body(per, n_dev, guess_v, sums_ref, ahead_ref, v_prev, state_in,
              guess_ref, out_ref, tridiag_ref, sem):
    guess_copy = pltpu.make_async_copy(guess_v, guess_ref, sem)
    guess_copy.start()
    acc = sums_ref[0]
    for k in range(1, n_dev):
        acc = acc + sums_ref[k]
    a, b, c, d = (jnp.sum(acc[q : q + 1, :], axis=1, keepdims=True) for q in range(4))
    inv_count = state_in[0:1, 0:1]
    alpha = a * inv_count
    late = alpha - state_in[1:2, 0:1]
    norm = jnp.maximum(b - 2.0 * late * c + late * late * d, 0.0)
    beta = jnp.sqrt(norm * inv_count + EPSILON)
    over = 1.0 / beta
    for s in range(per):
        out_ref[0, s] = ((ahead_ref[s] - late * v_prev[s]) * over).astype(BF16)
    lane = lax.broadcasted_iota(jnp.int32, (1, 128), 1)
    values = [state_in[2 + k : 3 + k, :] for k in range(3)] + [alpha]
    values += [state_in[6 + k : 7 + k, :] for k in range(3)] + [beta]
    line = jnp.zeros((1, 128), F32)
    for k, value in enumerate(values):
        line = jnp.where(lane == k, value, line)
    tridiag_ref[...] = line[:, :8]
    guess_copy.wait()


VMEM = pl.BlockSpec(memory_space=pltpu.VMEM)
SMEM = pl.BlockSpec(memory_space=pltpu.SMEM)
HBM = pl.BlockSpec(memory_space=pltpu.HBM)


def call(body, outs, operands, name, scratch=()):
    return pl.pallas_call(
        body,
        out_shape=[jax.ShapeDtypeStruct(shape, dtype) for _, shape, dtype in outs],
        in_specs=[spec for spec, _ in operands],
        out_specs=[spec for spec, _, _ in outs],
        scratch_shapes=list(scratch),
        compiler_params=pltpu.CompilerParams(vmem_limit_bytes=24 << 20),
        name=name,
    )(*[array for _, array in operands])


def on_device(
    n_sec,
    n_dev,
    left_env,
    right_env,
    edge_left,
    edge_right,
    inverse_sv,
    basis,
    lengths,
    partner,
    energy_left,
    energy_right,
):
    per = edge_left.shape[1]
    n_w = left_env.shape[1]
    rows = per * 128 + TAIL
    cube = (VMEM, (per, 128, 128), F32)
    small = (VMEM, (16, 128), F32)
    copies = (VMEM, (SIDE, rows, 128), BF16)
    edge = (1, per, 128, 128)
    sent_edge = passed_along(edge_right, "sec", -1)
    routes = jnp.swapaxes(partner, 1, 2)[0]
    given = (lengths, routes, edge_right, edge_left, inverse_sv, basis, energy_left, energy_right)
    line = (1, per, 128)
    moved, own_edge, energy, state, places = call(
        functools.partial(prepare_body, per, n_w),
        [(VMEM, (per, 128, 128), BF16), (VMEM, edge, BF16), cube, small, (SMEM, (per, n_w), jnp.int32)],
        [(HBM, pltpu.with_memory_space_constraint(array, pltpu.HBM)) for array in given],
        "prepare",
        [
            pltpu.SMEM(lengths.shape, jnp.int32),
            pltpu.SMEM((per, n_w), jnp.int32),
            pltpu.VMEM(lengths.shape, jnp.int32),
            pltpu.VMEM(edge, BF16),
            pltpu.VMEM(line, F32),
            pltpu.VMEM(line, jnp.int32),
            pltpu.VMEM(line, F32),
            pltpu.VMEM(line, F32),
            pltpu.SemaphoreType.DMA((9,)),
        ],
    )
    send, merged = call(
        functools.partial(merge_body, per),
        [copies, cube],
        [(VMEM, sent_edge), (VMEM, own_edge), (VMEM, moved), (VMEM, energy)],
        "merge",
    )
    for step in range(ITERS):
        whole = gathered(send, n_sec)
        body = functools.partial(step_body, step, per, n_w, n_dev)
        common = [(SMEM, places)]
        common += [(VMEM, array) for array in (whole, left_env, right_env, energy, state)]
        if step == 0:
            guess, send, vector, image, state = call(
                body,
                [(VMEM, edge, BF16), copies, cube, cube, small],
                common + [(VMEM, merged)],
                "step_first",
            )
        elif step < ITERS - 1:
            send, vector, image, state = call(
                body,
                [copies, cube, cube, small],
                common + [(VMEM, vector), (VMEM, image)],
                "step_next",
            )
        else:
            sums, ahead, vector, state = call(
                body,
                [(VMEM, (n_dev, 8, 128), F32), cube, cube, small],
                common + [(VMEM, vector), (VMEM, image)],
                "step_last",
            )
    sums = lax.all_to_all(sums, "tile", 0, 0, tiled=True)
    guess, last, tridiag = call(
        functools.partial(last_body, per, n_dev),
        [(HBM, edge, BF16), (VMEM, edge, BF16), (VMEM, (1, 8), F32)],
        [(VMEM, array) for array in (guess, sums, ahead, vector, state)],
        "finish",
        [pltpu.SemaphoreType.DMA],
    )
    return guess, last, tridiag


def solution(mesh):
    placed = (
        P("sec", None, "tile", None, None),
        P("sec", None, "tile", None, None),
        P("sec", "tile", None, None),
        P("sec", "tile", None, None),
        P("sec", "tile", None),
        P("sec", "tile", None),
        P("sec", None),
        P("sec", None, "tile"),
        P("sec", "tile", None),
        P("sec", "tile", None),
    )
    return jax.shard_map(
        functools.partial(on_device, mesh.shape["sec"], mesh.shape["tile"]),
        mesh=mesh,
        in_specs=placed,
        out_specs=(P("sec", "tile", None, None), P("sec", "tile", None, None), P("sec", None)),
        check_vma=False,
    )
```
